32 devices in a mesh: blk: 16 (over z, x, core), sub: 2 (over y).
Axes of the slice: x: 2, y: 2, z: 4, core: 2. Of those that a mesh axis runs over, the one named last changes fastest.
Arguments:
- vectors: bfloat16 [16, 131072], P('sub', 'blk')
- energies: float32 [131072], P('blk'), may hold values from 1 to 4
- tile_values: bfloat16 [16, 128, 128, 128], P('blk', 'sub'), may hold values from -0.1875 to 0.1875
- tile_rows: int32 [16, 128], P('blk', 'sub'), may hold values from 0 to 63
- tile_cols: int32 [16, 128], P('blk', 'sub'), may hold values from 0 to 63
- tile_offsets: int32 [16, 128], P('blk', 'sub'), may hold values from 0 to 2, as said below
- tile_count: int32 [16, 2], P('blk', 'sub'), may hold values from 8 to 64, as said below
Outputs:
- residual: float32 [16, 131072], P('sub', 'blk')
The draws below stay inside these ranges and needn't reach their ends.
Inputs may be any that keep to these rules, and one draw needn't show every extreme that they name: `tile_offsets`: an offset never exceeds the row block's index b; where the offset is 0, tile_rows >= tile_cols. `tile_count`: each count is 64 divided by 1, 2, 4 or 8.
All inputs are finite; a program needn't handle non-finite values.
Results may differ from the reference program's by a relative error of at most 0.0003.
Values may be sent and summed in bfloat16 or wider, within the bound.
No kernel may reach another device: no remote copies, remote signals or barrier semaphores. Data moves between devices by JAX's collectives and lax.ppermute only.
A program may use at most 64 MiB of HBM per device.

```python
import math
import jax
import jax.numpy as jnp
from jax import lax

VEC = 16
TS = 128
BW = 2
RT = 64
TL = 64
ROWS = 131072
N_BLK = 16
N_SUB = 2


def tile_triple(key):
    base = jax.random.fold_in(key, 11)
    key_rows, key_cols, key_offsets = jax.random.split(base, 3)
    shape = (N_BLK, N_SUB * TL)
    row_tile = jax.random.randint(key_rows, shape, 0, RT)
    col_tile = jax.random.randint(key_cols, shape, 0, RT)
    offset = jax.random.randint(key_offsets, shape, 0, BW + 1)
    device = lax.broadcasted_iota(jnp.int32, shape, 0)
    offset = jnp.minimum(offset, device)
    upper = jnp.maximum(row_tile, col_tile)
    lower = jnp.minimum(row_tile, col_tile)
    rows = jnp.where(offset == 0, upper, row_tile)
    cols = jnp.where(offset == 0, lower, col_tile)
    return (rows.astype(jnp.int32), cols.astype(jnp.int32), offset.astype(jnp.int32))


def draw_tile_rows(key, part):
    return tile_triple(key)[0]


def draw_tile_cols(key, part):
    return tile_triple(key)[1]


def draw_tile_offsets(key, part):
    return tile_triple(key)[2]


def draw_tile_count(key, part):
    base = jax.random.fold_in(key, 23)
    key_exp, key_top, key_low = jax.random.split(base, 3)
    total = N_BLK * N_SUB
    exponent = jax.random.randint(key_exp, (total,), 0, 4)
    counts = TL // jnp.left_shift(jnp.ones((total,), jnp.int32), exponent)
    top_place = jax.random.randint(key_top, (), 0, total)
    low_place = (top_place + 1 + jax.random.randint(key_low, (), 0, total - 1)) % total
    counts = counts.at[top_place].set(TL)
    counts = counts.at[low_place].set(TL // 8)
    return counts.reshape(N_BLK, N_SUB).astype(jnp.int32)


def draw_vectors(key, part):
    base = jax.random.fold_in(key, 37)
    key_main = jax.random.fold_in(base, 0)
    position = jnp.arange(ROWS, dtype=jnp.float32)
    ramp = 1.0 + 2.0 * position / (ROWS - 1)
    values = jax.random.normal(key_main, (VEC, ROWS), jnp.float32)
    return (values * ramp[None, :]).astype(jnp.bfloat16)


def steps_of(key, dims, cuts, low, largest):
    loudness = 1.0
    for dim, parts in cuts:
        steps = jax.random.uniform(jax.random.fold_in(jax.random.fold_in(key, 6), dim), (parts,), jnp.float32, low / len(cuts), largest / len(cuts))
        loudness = loudness * jnp.repeat(jnp.exp(steps), dims[dim] // parts).reshape((-1,) + (1,) * (len(dims) - 1 - dim))
    return loudness


def noise(key, shape, scale, reach, cuts=(), held_as=jnp.bfloat16):
    array = scale * jax.random.normal(key, shape, jnp.float32)
    if cuts:
        array = array * steps_of(key, shape, cuts, -0.22, 0.18)
    return jnp.clip(array, -reach, reach).astype(held_as)


def setup_inputs(seed: int = 0) -> dict:
    keys = jax.random.split(jax.random.key(seed), 8)
    vectors = draw_vectors(jax.random.fold_in(keys[7], 71), 0)
    energies = jnp.clip(jnp.exp(math.log(4.0) - 1.3862944 * jax.random.uniform(keys[1], (ROWS,), jnp.float32) ** steps_of(keys[1], (ROWS,), ((0, 16),), -0.2, 0.2)), 1.0, 4.0)
    tile_values = noise(keys[2], (N_BLK, N_SUB * TL, TS, TS), (TS * 8) ** -0.5, 0.1875, ((0, 16), (1, 2)))
    tile_rows = draw_tile_rows(jax.random.fold_in(keys[7], 71), 0)
    tile_cols = draw_tile_cols(jax.random.fold_in(keys[7], 71), 0)
    tile_offsets = draw_tile_offsets(jax.random.fold_in(keys[7], 71), 0)
    tile_count = draw_tile_count(jax.random.fold_in(keys[7], 71), 0)
    return {"vectors": vectors, "energies": energies, "tile_values": tile_values, "tile_rows": tile_rows, "tile_cols": tile_cols, "tile_offsets": tile_offsets, "tile_count": tile_count}


def ritz_coefficients(gram, projected):
    lower = jnp.linalg.cholesky(gram)
    half = lax.linalg.triangular_solve(lower, projected, left_side=True, lower=True)
    return lax.linalg.triangular_solve(lower, half, left_side=True, lower=True, transpose_a=True)

def reference(vectors, energies, tile_values, tile_rows, tile_cols, tile_offsets, tile_count):
    width = vectors.shape[0]
    blocks = vectors.reshape(width, N_BLK, RT, TS)
    padded = jnp.concatenate([jnp.zeros((width, BW, RT, TS), vectors.dtype), blocks], 1)
    slot_ids = jnp.arange(N_SUB * TL, dtype=jnp.int32)
    which_sub = slot_ids // TL
    within = slot_ids % TL
    highest = lax.Precision.HIGHEST

    def one_block(index):
        tile_vals = tile_values[index].astype(jnp.float32)
        row_ids = tile_rows[index]
        col_ids = tile_cols[index]
        offset_ids = tile_offsets[index]
        live = (within < tile_count[index][which_sub]).astype(jnp.float32)
        window = lax.dynamic_slice_in_dim(padded, index, BW + 1, 1)
        sources = window[:, BW - offset_ids, col_ids, :].astype(jnp.float32)
        own_tiles = lax.dynamic_index_in_dim(blocks, index, 1, keepdims=False)[:, row_ids, :].astype(jnp.float32)
        direct_terms = jnp.einsum('tij,ctj->cti', tile_vals, sources, precision=highest)
        mirror_terms = jnp.einsum('tji,ctj->cti', tile_vals, own_tiles, precision=highest)
        tile_range = jnp.arange(RT, dtype=jnp.int32)
        row_hot = (row_ids[:, None] == tile_range[None, :]).astype(jnp.float32) * live[:, None]
        col_hot = (col_ids[:, None] == tile_range[None, :]).astype(jnp.float32) * live[:, None]
        depth_hot = (offset_ids[:, None] == jnp.arange(BW + 1, dtype=jnp.int32)[None, :]).astype(jnp.float32)
        direct = jnp.einsum('cti,tr->cri', direct_terms, row_hot, precision=highest)
        mirror = jnp.einsum('cti,tk,tr->kcri', mirror_terms, depth_hot, col_hot, precision=highest)
        return (direct, mirror)
    direct, mirror = lax.map(one_block, jnp.arange(N_BLK, dtype=jnp.int32))
    total = direct + mirror[:, 0]
    for offset in range(1, BW + 1):
        moved = jnp.concatenate([mirror[offset:, offset], jnp.zeros((offset, width, RT, TS), jnp.float32)], 0)
        total = total + moved
    applied = jnp.transpose(total, (1, 0, 2, 3)).reshape(width, N_BLK * RT * TS)
    vectors_wide = vectors.astype(jnp.float32)
    applied = applied + energies[None, :] * vectors_wide
    gram = jnp.dot(vectors.astype(jnp.float32), vectors.T.astype(jnp.float32), preferred_element_type=jnp.float32)
    projected = jnp.dot(vectors_wide, applied.T, precision=highest)
    coefficients = ritz_coefficients(gram, projected)
    return applied - jnp.dot(coefficients.T, vectors_wide, precision=highest)
```

```python
import functools

import jax
import jax.numpy as jnp
from jax import lax
from jax.experimental import pallas as pl
from jax.experimental.pallas import tpu as pltpu
from jax.sharding import PartitionSpec as P

BW = 2
GROUP = 8
F32 = jnp.float32
BF16 = jnp.bfloat16
I32 = jnp.int32
HBM = pl.BlockSpec(memory_space=pltpu.HBM)
VMEM = pl.BlockSpec(memory_space=pltpu.VMEM)
SMEM = pl.BlockSpec(memory_space=pltpu.SMEM)
NT = (((1,), (1,)), ((), ()))


def shifted(value, steps):
    count = lax.axis_size("blk")
    first, last = (max(0, -steps), min(count, count - steps))
    return lax.ppermute(value, "blk", [(source, source + steps) for source in range(first, last)])


def swap_sub(value):
    return lax.ppermute(value, "sub", [(0, 1), (1, 0)])


def swap_core(value):
    return lax.ppermute(value, "blk", [(i, i ^ 1) for i in range(lax.axis_size("blk"))])


def rounds_over(axis):
    count = lax.axis_size(axis)
    rounds, stride = [], 1
    while stride < count:
        rest = count // stride
        radix = next(p for p in range(2, rest + 1) if rest % p == 0)
        rounds.append((axis, stride, radix))
        stride *= radix
    return rounds


def run_rounds(value, rounds):
    for axis, stride, radix in rounds:
        total = value
        for turn in range(1, radix):
            pairs = []
            for source in range(lax.axis_size(axis)):
                digit = (source // stride) % radix
                pairs.append((source, source + ((digit + turn) % radix - digit) * stride))
            total = total + lax.ppermute(value, axis, pairs)
        value = total
    return value


def tile_at(index, side):
    return pl.ds(pl.multiple_of(index * side, side), side)


def split2(value):
    spread = value * 65537.0
    high = spread - (spread - value)
    return high, value - high


def odd_block():
    return lax.rem(lax.axis_index("blk"), 2) == 1


def in_order(own, other, out):
    rows = own.shape[0]
    first = lax.axis_index("sub") == 0

    @pl.when(first)
    def _():
        out[0:rows, :] = own[...]
        out[rows : 2 * rows, :] = other[...]

    @pl.when(jnp.logical_not(first))
    def _():
        out[0:rows, :] = other[...]
        out[rows : 2 * rows, :] = own[...]


def load_kernel(source, target, sem):
    copy = pltpu.make_async_copy(source, target, sem)
    copy.start()
    copy.wait()


def join_kernel(own, other, below, out):
    in_order(own, other, out)


def join_below_kernel(own, other, whole, term, out, across, later):
    in_order(own, other, out)
    later[...] = term[...]
    odd = odd_block()

    @pl.when(odd)
    def _():
        across[...] = out[...]

    @pl.when(jnp.logical_not(odd))
    def _():
        across[...] = whole[...]


def levels_at(energies, start, step):
    side = energies.shape[1]
    rows = [energies[pl.ds((start + i) // side, 1), :] for i in range(0, step, side)]
    return jnp.concatenate(rows, 1)


def mirror_kernel(table, vec, energies, tiles, m0, m1, m2, small, acc):
    side = tiles.shape[-1]
    width, rows_dev = vec.shape
    acc[...] = jnp.zeros_like(acc)

    @pl.loop(0, table[3, 0] // GROUP)
    def _(group):
        for lane in range(GROUP):
            slot = group * GROUP + lane
            term = jnp.dot(
                vec[:, tile_at(table[0, slot], side)], tiles[slot], preferred_element_type=F32
            )
            acc[table[2, slot], :, tile_at(table[1, slot], side)] += term

    m0[...] = acc[0]
    m1[...] = acc[1]
    m2[...] = acc[2]
    total = jnp.zeros((width, 3 * width), F32)
    step = 2 * side
    for start in range(0, rows_dev, step):
        v = vec[:, pl.ds(start, step)]
        scaled = split2(levels_at(energies, start, step) * v.astype(F32))
        total += lax.dot_general(
            v,
            jnp.concatenate([v] + [part.astype(BF16) for part in scaled], 0),
            NT,
            preferred_element_type=F32,
        )
    total *= 1.0 / lax.axis_size("sub")
    small[0:width, 0:width] = total[:, :width]
    small[width : 2 * width, 0:width] = total[:, width : 2 * width] + total[:, 2 * width :]


def write_parts(columns, value, targets):
    if len(targets) == 1:
        targets[0][...] = value(slice(None))
        return
    mine = lax.axis_index("sub") * columns
    for start, target in zip((mine, columns - mine), targets):
        target[...] = value(pl.ds(pl.multiple_of(start, columns), columns))


def up_kernel(columns, m2, crossed, *targets):
    odd = odd_block()

    @pl.when(odd)
    def _():
        write_parts(columns, lambda rows: m2[rows, :] + crossed[rows, :], targets)

    @pl.when(jnp.logical_not(odd))
    def _():
        write_parts(columns, lambda rows: m2[rows, :], targets)


def sum_kernel(first, second, small, out, later):
    out[...] = first[...] + second[...]
    later[...] = small[...]


def direct_kernel(
    columns, table, vec, vec1, vec2, tiles, m0, crossed, before, *rest
):
    targets, (small, sources, own) = rest[:-3], rest[-3:]
    side = tiles.shape[-1]
    width, rows_dev = vec.shape
    own[...] = jnp.zeros_like(own)
    sources[0] = vec[...]
    sources[1] = vec1[...]
    sources[2] = vec2[...]

    @pl.loop(0, table[3, 0] // GROUP)
    def _(group):
        for lane in range(GROUP):
            slot = group * GROUP + lane
            term = lax.dot_general(
                sources[table[2, slot], :, tile_at(table[1, slot], side)],
                tiles[slot],
                NT,
                preferred_element_type=F32,
            )
            own[:, tile_at(table[0, slot], side)] += term

    left = jnp.zeros((width, 2 * width), F32)
    right = jnp.zeros((2 * width, width), F32)
    step = 2 * side
    for start in range(0, rows_dev, step):
        here = pl.ds(start, step)
        v = vec[:, here]
        parts = jnp.concatenate([part.astype(BF16) for part in split2(own[:, here])], 0)
        left += lax.dot_general(v, parts, NT, preferred_element_type=F32)
        right += lax.dot_general(parts, v, NT, preferred_element_type=F32)
    small[0:width, 0:width] = before[0:width, 0:width]
    small[width : 2 * width, 0:width] = before[width : 2 * width, 0:width] + (
        (left[:, :width] + left[:, width:]) + (right[:width] + right[width:])
    )
    odd = odd_block()

    @pl.when(odd)
    def _():
        write_parts(columns, lambda part: own[part, :] + m0[part, :], targets)

    @pl.when(jnp.logical_not(odd))
    def _():
        write_parts(
            columns, lambda part: own[part, :] + (m0[part, :] + crossed[part, :]), targets
        )


def eliminate(system):
    width = system.shape[1]
    col_id = lax.broadcasted_iota(I32, system.shape, 1)
    for pivot in range(width):
        column = system[:, pivot : pivot + 1] / system[pivot : pivot + 1, pivot : pivot + 1]
        row = system[pivot : pivot + 1, :]
        system = jnp.where(col_id == pivot, column, system - column * row)
    return system[width:, :]


def final_kernel(small, vec, mine, energies, *rest):
    terms, (out, coeffs) = rest[:-2], rest[-2:]
    width, rows_dev = vec.shape
    columns = mine.shape[0]
    side = energies.shape[1]
    coeffs[...] = eliminate(small[:, :width])
    wanted = coeffs[pl.ds(lax.axis_index("sub") * columns, columns), :]
    high, rest_of = split2(wanted)
    mid, low = split2(rest_of)
    factors = jnp.concatenate([high, mid, low], 0).astype(BF16)
    step = 8 * side
    for start in range(0, rows_dev, step):
        here = pl.ds(start, step)
        model = jnp.dot(factors, vec[:, here], preferred_element_type=F32)
        model = model[:columns] + (model[columns : 2 * columns] + model[2 * columns :])
        applied = levels_at(energies, start, step) * mine[:, here].astype(F32)
        for term in terms:
            applied = applied + term[:, here]
        out[:, here] = applied - model


def call(kernel, name, out_shape, in_specs, out_specs, args, cycles, scratch=(), room=24):
    return pl.pallas_call(
        kernel,
        out_shape=out_shape,
        in_specs=in_specs,
        out_specs=out_specs,
        scratch_shapes=list(scratch),
        compiler_params=pltpu.CompilerParams(vmem_limit_bytes=room * 1024 * 1024),
        cost_estimate=pl.CostEstimate(
            flops=0, bytes_accessed=cycles * 3_000_000, transcendentals=0
        ),
        name=name,
    )(*args)


def on_device(vectors, energies, tile_values, tile_rows, tile_cols, tile_offsets, tile_count):
    columns, rows_dev = vectors.shape
    n_sub = lax.axis_size("sub")
    pair = n_sub == 2
    width = columns * n_sub
    slots, side = tile_values.shape[1:3]
    levels = energies.reshape(rows_dev // side, side)
    narrow = jax.ShapeDtypeStruct((width, rows_dev), BF16)
    block = jax.ShapeDtypeStruct((width, rows_dev), F32)
    half = jax.ShapeDtypeStruct((columns, rows_dev), F32)
    square = jax.ShapeDtypeStruct((2 * width, side), F32)
    parts = [half] * 2 if pair else [block]

    table = jnp.concatenate(
        [tile_rows, tile_cols, tile_offsets, jnp.broadcast_to(tile_count, tile_rows.shape)], 0
    )
    tiles = call(
        load_kernel,
        "load",
        jax.ShapeDtypeStruct((slots, side, side), BF16),
        [HBM],
        VMEM,
        (tile_values.reshape(slots, side, side),),
        1,
        [pltpu.SemaphoreType.DMA],
        60,
    )
    if pair:
        other = swap_sub(vectors)
        below = shifted(vectors, BW)
        whole = call(join_kernel, "join", narrow, [VMEM] * 3, VMEM, (vectors, other, below), 1)
    else:
        whole = lax.all_gather(vectors, "sub", axis=0, tiled=True)
    m0, m1, m2, before = call(
        mirror_kernel,
        "mirror",
        [block] * 3 + [square],
        [SMEM] + [VMEM] * 3,
        [VMEM] * 4,
        (table, whole, levels, tiles),
        2,
        [pltpu.VMEM((BW + 1, width, rows_dev), F32)],
    )
    if pair:
        whole2, across, m1 = call(
            join_below_kernel,
            "join_below",
            [narrow] * 2 + [block],
            [VMEM] * 4,
            [VMEM] * 3,
            (below, swap_sub(below), whole, m1),
            1,
        )
    else:
        whole2 = shifted(whole, BW)
        across = jnp.where(lax.rem(lax.axis_index("blk"), 2) == 1, whole2, whole)
    whole1 = swap_core(across)
    crossed = swap_core(m1)
    up = call(
        functools.partial(up_kernel, columns),
        "up",
        parts,
        [VMEM] * 2,
        [VMEM] * len(parts),
        (m2, crossed),
        1,
    )
    *own, small = call(
        functools.partial(direct_kernel, columns),
        "direct",
        parts + [square],
        [SMEM] + [VMEM] * 7,
        [VMEM] * (len(parts) + 1),
        (table, whole, whole1, whole2, tiles, m0, crossed, before),
        3,
        [pltpu.VMEM((BW + 1, width, rows_dev), BF16), pltpu.VMEM((width, rows_dev), F32)],
    )
    rounds = rounds_over("blk")
    small = run_rounds(small, rounds[:2])
    if pair:
        up, small = call(
            sum_kernel,
            "sum",
            [half, square],
            [VMEM] * 3,
            [VMEM] * 2,
            (up[0], swap_sub(up[1]), small),
            1,
        )
        terms = [own[0], swap_sub(own[1])]
    else:
        up = lax.psum_scatter(up[0], "sub", scatter_dimension=0, tiled=True)
        terms = [lax.psum_scatter(own[0], "sub", scatter_dimension=0, tiled=True)]
    terms.append(shifted(up, -BW))
    small = run_rounds(small, rounds_over("sub") + rounds[2:])
    return call(
        final_kernel,
        "final",
        half,
        [VMEM] * (4 + len(terms)),
        VMEM,
        (small, whole, vectors, levels, *terms),
        2,
        [pltpu.VMEM((width, width), F32)],
    )


def solution(mesh):
    in_specs = (
        P("sub", "blk"),
        P("blk"),
        P("blk", "sub", None, None),
        P("blk", "sub"),
        P("blk", "sub"),
        P("blk", "sub"),
        P("blk", "sub"),
    )
    out_specs = P("sub", "blk")
    return jax.shard_map(
        on_device, mesh=mesh, in_specs=in_specs, out_specs=out_specs, check_vma=False
    )
```

```python
import functools

import jax
import jax.numpy as jnp
from jax import lax
from jax.experimental import pallas as pl
from jax.experimental.pallas import tpu as pltpu
from jax.sharding import PartitionSpec as P

BW = 2
GROUP = 16
LIVE_UNIT = 65536
F32 = jnp.float32
BF16 = jnp.bfloat16
I32 = jnp.int32
ANY = pl.BlockSpec(memory_space=pl.ANY)
HBM = pl.BlockSpec(memory_space=pltpu.HBM)
VMEM = pl.BlockSpec(memory_space=pltpu.VMEM)
SMEM = pl.BlockSpec(memory_space=pltpu.SMEM)
NT = (((1,), (1,)), ((), ()))


def shifted(value, steps):
    count = lax.axis_size("blk")
    first, last = (max(0, -steps), min(count, count - steps))
    return lax.ppermute(value, "blk", [(source, source + steps) for source in range(first, last)])


def swap_sub(value):
    return lax.ppermute(value, "sub", [(0, 1), (1, 0)])


def swap_core(value):
    return lax.ppermute(value, "blk", [(i, i ^ 1) for i in range(lax.axis_size("blk"))])


def rounds_over(axis):
    count = lax.axis_size(axis)
    rounds, stride = [], 1
    while stride < count:
        rest = count // stride
        radix = next(p for p in range(2, rest + 1) if rest % p == 0)
        rounds.append((axis, stride, radix))
        stride *= radix
    return rounds


def run_rounds(value, rounds):
    for axis, stride, radix in rounds:
        total = value
        for turn in range(1, radix):
            pairs = []
            for source in range(lax.axis_size(axis)):
                digit = (source // stride) % radix
                pairs.append((source, source + ((digit + turn) % radix - digit) * stride))
            total = total + lax.ppermute(value, axis, pairs)
        value = total
    return value


def tile_at(index, side):
    return pl.ds(pl.multiple_of(index * side, side), side)


def split2(value):
    spread = value * 65537.0
    high = spread - (spread - value)
    return high, value - high


def odd_block():
    return lax.rem(lax.axis_index("blk"), 2) == 1


def in_order(own, other, out):
    rows = own.shape[0]
    first = lax.axis_index("sub") == 0

    @pl.when(first)
    def _():
        out[0:rows, :] = own[...]
        out[rows : 2 * rows, :] = other[...]

    @pl.when(jnp.logical_not(first))
    def _():
        out[0:rows, :] = other[...]
        out[rows : 2 * rows, :] = own[...]


def load_kernel(source, target, sem):
    copy = pltpu.make_async_copy(source, target, sem)
    copy.start()
    copy.wait()


def add_terms(table, slots, term_of, total, place):
    count = table[0, 0] // LIVE_UNIT
    group_size = min(GROUP, slots)

    @pl.loop(0, pl.cdiv(count, group_size))
    def _(group):
        first = group * group_size
        terms = [term_of(first + lane) for lane in range(group_size)]
        for lane, term in enumerate(terms):
            live = first + lane < count
            total[place(first + lane)] += jnp.where(live, term, 0.0)


def join_kernel(own, other, below, out):
    in_order(own, other, out)


def join_below_kernel(own, other, whole, term, out, across, later):
    in_order(own, other, out)
    later[...] = term[...]
    odd = odd_block()

    @pl.when(odd)
    def _():
        across[...] = out[...]

    @pl.when(jnp.logical_not(odd))
    def _():
        across[...] = whole[...]


def levels_at(energies, start, step):
    side = energies.shape[1]
    rows = [energies[pl.ds((start + i) // side, 1), :] for i in range(0, step, side)]
    return jnp.concatenate(rows, 1)


def mirror_kernel(table, vec, energies, tiles, m0, m1, m2, small, acc):
    side = tiles.shape[-1]
    width, rows_dev = vec.shape
    acc[...] = jnp.zeros_like(acc)

    add_terms(
        table,
        tiles.shape[0],
        lambda slot: jnp.dot(
            vec[:, tile_at(table[0, slot] % LIVE_UNIT, side)], tiles[slot], preferred_element_type=F32
        ),
        acc,
        lambda slot: (table[2, slot], slice(None), tile_at(table[1, slot], side)),
    )
    m0[...] = acc[0]
    m1[...] = acc[1]
    m2[...] = acc[2]
    total = jnp.zeros((width, 3 * width), F32)
    step = 2 * side
    for start in range(0, rows_dev, step):
        v = vec[:, pl.ds(start, step)]
        scaled = split2(levels_at(energies, start, step) * v.astype(F32))
        total += lax.dot_general(
            v,
            jnp.concatenate([v] + [part.astype(BF16) for part in scaled], 0),
            NT,
            preferred_element_type=F32,
        )
    total *= 1.0 / lax.axis_size("sub")
    small[0:width, 0:width] = total[:, :width]
    small[width : 2 * width, 0:width] = total[:, width : 2 * width] + total[:, 2 * width :]


def write_parts(columns, value, targets):
    if len(targets) == 1:
        targets[0][...] = value(slice(None))
        return
    mine = lax.axis_index("sub") * columns
    for start, target in zip((mine, columns - mine), targets):
        target[...] = value(pl.ds(pl.multiple_of(start, columns), columns))


def up_kernel(columns, m2, crossed, ready, *targets):
    odd = odd_block()

    @pl.when(odd)
    def _():
        write_parts(columns, lambda rows: m2[rows, :] + crossed[rows, :], targets)

    @pl.when(jnp.logical_not(odd))
    def _():
        write_parts(columns, lambda rows: m2[rows, :], targets)


def sum_kernel(first, second, ready, out):
    out[...] = first[...] + second[...]


def direct_kernel(
    columns, table, vec, vec1, vec2, tiles, m0, crossed, before, *rest
):
    targets, (small, sources, own) = rest[:-3], rest[-3:]
    side = tiles.shape[-1]
    width, rows_dev = vec.shape
    own[...] = jnp.zeros_like(own)
    sources[0] = vec[...]
    sources[1] = vec1[...]
    sources[2] = vec2[...]

    add_terms(
        table,
        tiles.shape[0],
        lambda slot: lax.dot_general(
            sources[table[2, slot], :, tile_at(table[1, slot], side)],
            tiles[slot],
            NT,
            preferred_element_type=F32,
        ),
        own,
        lambda slot: (slice(None), tile_at(table[0, slot] % LIVE_UNIT, side)),
    )
    left = jnp.zeros((width, 2 * width), F32)
    right = jnp.zeros((2 * width, width), F32)
    step = 2 * side
    for start in range(0, rows_dev, step):
        here = pl.ds(start, step)
        v = vec[:, here]
        parts = jnp.concatenate([part.astype(BF16) for part in split2(own[:, here])], 0)
        left += lax.dot_general(v, parts, NT, preferred_element_type=F32)
        right += lax.dot_general(parts, v, NT, preferred_element_type=F32)
    small[0:width, 0:width] = before[0:width, 0:width]
    small[width : 2 * width, 0:width] = before[width : 2 * width, 0:width] + (
        (left[:, :width] + left[:, width:]) + (right[:width] + right[width:])
    )
    odd = odd_block()

    @pl.when(odd)
    def _():
        write_parts(columns, lambda part: own[part, :] + m0[part, :], targets)

    @pl.when(jnp.logical_not(odd))
    def _():
        write_parts(
            columns, lambda part: own[part, :] + (m0[part, :] + crossed[part, :]), targets
        )


def eliminate(system):
    width = system.shape[1]
    col_id = lax.broadcasted_iota(I32, system.shape, 1)
    for pivot in range(0, width, 2):
        col0, col1 = [
            jnp.broadcast_to(system[:, i : i + 1], system.shape) for i in (pivot, pivot + 1)
        ]
        row0, row1 = [
            jnp.broadcast_to(system[i : i + 1, :], system.shape) for i in (pivot, pivot + 1)
        ]
        a, c, b, d = [
            jnp.broadcast_to(col[i : i + 1, :], system.shape)
            for col in (col0, col1)
            for i in (pivot, pivot + 1)
        ]
        ratio = b / a
        new1 = (col1 - col0 * ratio) / (d - c * ratio)
        new0 = col0 / a - new1 * (c / a)
        system = system - (new0 * row0 + new1 * row1)
        system = jnp.where(col_id == pivot, new0, jnp.where(col_id == pivot + 1, new1, system))
    return system[width:, :]


def model_kernel(small, vec, mine, energies, *rest):
    terms, (out, coeffs) = rest[:-2], rest[-2:]
    width, rows_dev = vec.shape
    columns = mine.shape[0]
    side = energies.shape[1]
    coeffs[...] = eliminate(small[:, :width])
    wanted = coeffs[pl.ds(lax.axis_index("sub") * columns, columns), :]
    high, rest_of = split2(wanted)
    mid, low = split2(rest_of)
    factors = jnp.concatenate([high, mid, low], 0).astype(BF16)
    step = 8 * side
    for start in range(0, rows_dev, step):
        here = pl.ds(start, step)
        model = jnp.dot(factors, vec[:, here], preferred_element_type=F32)
        model = model[:columns] + (model[columns : 2 * columns] + model[2 * columns :])
        applied = levels_at(energies, start, step) * mine[:, here].astype(F32)
        for term in terms:
            applied = applied + term[:, here]
        out[:, here] = applied - model


def last_kernel(first, second, out):
    out[...] = first[...] + second[...]


def call(kernel, name, out_shape, in_specs, out_specs, args, cycles, scratch=(), room=24):
    return pl.pallas_call(
        kernel,
        out_shape=out_shape,
        in_specs=in_specs,
        out_specs=out_specs,
        scratch_shapes=list(scratch),
        compiler_params=pltpu.CompilerParams(vmem_limit_bytes=room * 1024 * 1024),
        cost_estimate=pl.CostEstimate(
            flops=0, bytes_accessed=cycles * 3_000_000, transcendentals=0
        ),
        name=name,
    )(*args)


def on_device(vectors, energies, tile_values, tile_rows, tile_cols, tile_offsets, tile_count):
    columns, rows_dev = vectors.shape
    n_sub = lax.axis_size("sub")
    pair = n_sub == 2
    width = columns * n_sub
    slots, side = tile_values.shape[1:3]
    levels = energies.reshape(rows_dev // side, side)
    narrow = jax.ShapeDtypeStruct((width, rows_dev), BF16)
    block = jax.ShapeDtypeStruct((width, rows_dev), F32)
    half = jax.ShapeDtypeStruct((columns, rows_dev), F32)
    square = jax.ShapeDtypeStruct((2 * width, side), F32)
    parts = [half] * 2 if pair else [block]

    table = jnp.concatenate(
        [tile_rows + LIVE_UNIT * tile_count, tile_cols, tile_offsets], 0
    )
    tiles = call(
        load_kernel,
        "load",
        jax.ShapeDtypeStruct((slots, side, side), BF16),
        [HBM],
        VMEM,
        (tile_values.reshape(slots, side, side),),
        1,
        [pltpu.SemaphoreType.DMA],
        51,
    )
    if pair:
        other = swap_sub(vectors)
        below = shifted(vectors, BW)
        whole = call(join_kernel, "join", narrow, [VMEM] * 3, VMEM, (vectors, other, below), 1)
    else:
        whole = lax.all_gather(vectors, "sub", axis=0, tiled=True)
    m0, m1, m2, before = call(
        mirror_kernel,
        "mirror",
        [block] * 3 + [square],
        [SMEM] + [VMEM] * 3,
        [VMEM] * 4,
        (table, whole, levels, tiles),
        2,
        [pltpu.VMEM((BW + 1, width, rows_dev), F32)],
    )
    if pair:
        whole2, across, m1 = call(
            join_below_kernel,
            "join_below",
            [narrow] * 2 + [block],
            [VMEM] * 4,
            [VMEM] * 3,
            (below, swap_sub(below), whole, m1),
            1,
        )
    else:
        whole2 = shifted(whole, BW)
        across = jnp.where(lax.rem(lax.axis_index("blk"), 2) == 1, whole2, whole)
    whole1 = swap_core(across)
    crossed = swap_core(m1)
    up = call(
        functools.partial(up_kernel, columns),
        "up",
        parts,
        [VMEM] * 2 + [ANY],
        [VMEM] * len(parts),
        (m2, crossed, m2),
        1,
    )
    *own, small = call(
        functools.partial(direct_kernel, columns),
        "direct",
        parts + [square],
        [SMEM] + [VMEM] * 7,
        [VMEM] * (len(parts) + 1),
        (table, whole, whole1, whole2, tiles, m0, crossed, before),
        3,
        [pltpu.VMEM((BW + 1, width, rows_dev), BF16), pltpu.VMEM((width, rows_dev), F32)],
    )
    first, *others = rounds_over("blk")
    rounds = others + [first] + rounds_over("sub")
    stages = [small]
    for one in rounds:
        stages.append(run_rounds(stages[-1], [one]))
    small = stages[-1]
    if pair:
        up = call(
            sum_kernel,
            "sum",
            half,
            [VMEM] * 2 + [ANY],
            VMEM,
            (up[0], swap_sub(up[1]), stages[len(others)]),
            1,
        )
        terms = [own[0], swap_sub(own[1])]
    else:
        up = lax.psum_scatter(up[0], "sub", scatter_dimension=0, tiled=True)
        terms = [lax.psum_scatter(own[0], "sub", scatter_dimension=0, tiled=True)]
    nearly = call(
        model_kernel,
        "model",
        half,
        [VMEM] * (4 + len(terms)),
        VMEM,
        (small, whole, vectors, levels, *terms),
        2,
        [pltpu.VMEM((width, width), F32)],
    )
    return call(last_kernel, "last", half, [VMEM] * 2, VMEM, (nearly, shifted(up, -BW)), 1)


def solution(mesh):
    in_specs = (
        P("sub", "blk"),
        P("blk"),
        P("blk", "sub", None, None),
        P("blk", "sub"),
        P("blk", "sub"),
        P("blk", "sub"),
        P("blk", "sub"),
    )
    out_specs = P("sub", "blk")
    return jax.shard_map(
        on_device, mesh=mesh, in_specs=in_specs, out_specs=out_specs, check_vma=False
    )
```

```python
import functools

import jax
import jax.numpy as jnp
from jax import lax
from jax.experimental import pallas as pl
from jax.experimental.pallas import tpu as pltpu
from jax.sharding import PartitionSpec as P

BW = 2
GROUP = 64
LIVE_UNIT = 65536
F32 = jnp.float32
BF16 = jnp.bfloat16
I32 = jnp.int32
ANY = pl.BlockSpec(memory_space=pl.ANY)
HBM = pl.BlockSpec(memory_space=pltpu.HBM)
VMEM = pl.BlockSpec(memory_space=pltpu.VMEM)
SMEM = pl.BlockSpec(memory_space=pltpu.SMEM)
NT = (((1,), (1,)), ((), ()))


def shifted(value, steps):
    count = lax.axis_size("blk")
    first, last = (max(0, -steps), min(count, count - steps))
    return lax.ppermute(value, "blk", [(source, source + steps) for source in range(first, last)])


def swap_sub(value):
    return lax.ppermute(value, "sub", [(0, 1), (1, 0)])


def swap_core(value):
    return lax.ppermute(value, "blk", [(i, i ^ 1) for i in range(lax.axis_size("blk"))])


def rounds_over(axis):
    count = lax.axis_size(axis)
    rounds, stride = [], 1
    while stride < count:
        rest = count // stride
        radix = next(p for p in range(2, rest + 1) if rest % p == 0)
        rounds.append((axis, stride, radix))
        stride *= radix
    return rounds


def run_rounds(value, rounds):
    for axis, stride, radix in rounds:
        total = value
        for turn in range(1, radix):
            pairs = []
            for source in range(lax.axis_size(axis)):
                digit = (source // stride) % radix
                pairs.append((source, source + ((digit + turn) % radix - digit) * stride))
            total = total + lax.ppermute(value, axis, pairs)
        value = total
    return value


def tile_at(index, side):
    return pl.ds(pl.multiple_of(index * side, side), side)


def split2(value):
    spread = value * 65537.0
    high = spread - (spread - value)
    return high, value - high


def odd_block():
    return lax.rem(lax.axis_index("blk"), 2) == 1


def in_order(own, other, out):
    rows = own.shape[0]
    first = lax.axis_index("sub") == 0

    @pl.when(first)
    def _():
        out[0:rows, :] = own[...]
        out[rows : 2 * rows, :] = other[...]

    @pl.when(jnp.logical_not(first))
    def _():
        out[0:rows, :] = other[...]
        out[rows : 2 * rows, :] = own[...]


def load_kernel(source, target, sem):
    copy = pltpu.make_async_copy(source, target, sem)
    copy.start()
    copy.wait()


def add_terms(table, slots, term_of, total, place, unrolled=False):
    count = table[0, 0] // LIVE_UNIT
    group_size = min(GROUP, slots)

    def add_group(group):
        first = group * group_size
        terms = [term_of(first + lane) for lane in range(group_size)]
        for lane, term in enumerate(terms):
            live = first + lane < count
            total[place(first + lane)] += jnp.where(live, term, 0.0)

    if unrolled and group_size == slots:
        add_group(0)
    else:
        pl.loop(0, pl.cdiv(count, group_size))(add_group)


def join_kernel(own, other, below, out):
    in_order(own, other, out)


def join_below_kernel(own, other, whole, term, out, across, later):
    in_order(own, other, out)
    later[...] = term[...]
    odd = odd_block()

    @pl.when(odd)
    def _():
        across[...] = out[...]

    @pl.when(jnp.logical_not(odd))
    def _():
        across[...] = whole[...]


def levels_at(energies, start, step):
    side = energies.shape[1]
    rows = [energies[pl.ds((start + i) // side, 1), :] for i in range(0, step, side)]
    return jnp.concatenate(rows, 1)


def mirror_kernel(table, vec, energies, tiles, m0, m1, m2, small, acc):
    side = tiles.shape[-1]
    width, rows_dev = vec.shape
    acc[...] = jnp.zeros_like(acc)

    add_terms(
        table,
        tiles.shape[0],
        lambda slot: jnp.dot(
            vec[:, tile_at(table[0, slot] % LIVE_UNIT, side)], tiles[slot], preferred_element_type=F32
        ),
        acc,
        lambda slot: (table[2, slot], slice(None), tile_at(table[1, slot], side)),
        unrolled=True,
    )
    m0[...] = acc[0]
    m1[...] = acc[1]
    m2[...] = acc[2]
    total = jnp.zeros((width, 3 * width), F32)
    step = 2 * side
    for start in range(0, rows_dev, step):
        v = vec[:, pl.ds(start, step)]
        scaled = split2(levels_at(energies, start, step) * v.astype(F32))
        total += lax.dot_general(
            v,
            jnp.concatenate([v] + [part.astype(BF16) for part in scaled], 0),
            NT,
            preferred_element_type=F32,
        )
    total *= 1.0 / lax.axis_size("sub")
    small[0:width, 0:width] = total[:, :width]
    small[width : 2 * width, 0:width] = total[:, width : 2 * width] + total[:, 2 * width :]


def write_parts(columns, value, targets):
    if len(targets) == 1:
        targets[0][...] = value(slice(None))
        return
    mine = lax.axis_index("sub") * columns
    for start, target in zip((mine, columns - mine), targets):
        target[...] = value(pl.ds(pl.multiple_of(start, columns), columns))


def up_kernel(columns, m2, crossed, ready, *targets):
    odd = odd_block()

    @pl.when(odd)
    def _():
        write_parts(columns, lambda rows: m2[rows, :] + crossed[rows, :], targets)

    @pl.when(jnp.logical_not(odd))
    def _():
        write_parts(columns, lambda rows: m2[rows, :], targets)


def sum_kernel(first, second, ready, out):
    out[...] = first[...] + second[...]


def direct_kernel(
    columns, table, vec, vec1, vec2, tiles, m0, crossed, before, *rest
):
    targets, (small, sources, own) = rest[:-3], rest[-3:]
    side = tiles.shape[-1]
    width, rows_dev = vec.shape
    own[...] = jnp.zeros_like(own)
    sources[0] = vec[...]
    sources[1] = vec1[...]
    sources[2] = vec2[...]

    add_terms(
        table,
        tiles.shape[0],
        lambda slot: lax.dot_general(
            sources[table[2, slot], :, tile_at(table[1, slot], side)],
            tiles[slot],
            NT,
            preferred_element_type=F32,
        ),
        own,
        lambda slot: (slice(None), tile_at(table[0, slot] % LIVE_UNIT, side)),
    )
    left = jnp.zeros((width, 2 * width), F32)
    step = 2 * side
    for start in range(0, rows_dev, step):
        here = pl.ds(start, step)
        v = vec[:, here]
        parts = jnp.concatenate([part.astype(BF16) for part in split2(own[:, here])], 0)
        left += lax.dot_general(v, parts, NT, preferred_element_type=F32)
    cross = left[:, :width] + left[:, width:]
    small[0:width, 0:width] = before[0:width, 0:width]
    small[width : 2 * width, 0:width] = before[width : 2 * width, 0:width] + (
        cross + cross.T
    )
    odd = odd_block()

    @pl.when(odd)
    def _():
        write_parts(columns, lambda part: own[part, :] + m0[part, :], targets)

    @pl.when(jnp.logical_not(odd))
    def _():
        write_parts(
            columns, lambda part: own[part, :] + (m0[part, :] + crossed[part, :]), targets
        )


def eliminate(system):
    width = system.shape[1]
    col_id = lax.broadcasted_iota(I32, system.shape, 1)
    for pivot in range(0, width, 2):
        col0, col1 = [
            jnp.broadcast_to(system[:, i : i + 1], system.shape) for i in (pivot, pivot + 1)
        ]
        row0, row1 = [
            jnp.broadcast_to(system[i : i + 1, :], system.shape) for i in (pivot, pivot + 1)
        ]
        a, c, b, d = [
            jnp.broadcast_to(col[i : i + 1, :], system.shape)
            for col in (col0, col1)
            for i in (pivot, pivot + 1)
        ]
        ratio = b / a
        new1 = (col1 - col0 * ratio) / (d - c * ratio)
        new0 = col0 / a - new1 * (c / a)
        system = system - (new0 * row0 + new1 * row1)
        system = jnp.where(col_id == pivot, new0, jnp.where(col_id == pivot + 1, new1, system))
    return system[width:, :]


def model_kernel(small, vec, mine, energies, *rest):
    terms, (out, coeffs) = rest[:-2], rest[-2:]
    width, rows_dev = vec.shape
    columns = mine.shape[0]
    side = energies.shape[1]
    coeffs[...] = eliminate(small[:, :width])
    wanted = coeffs[pl.ds(lax.axis_index("sub") * columns, columns), :]
    high, rest_of = split2(wanted)
    mid, low = split2(rest_of)
    factors = jnp.concatenate([high, mid, low], 0).astype(BF16)
    step = 8 * side
    for start in range(0, rows_dev, step):
        here = pl.ds(start, step)
        model = jnp.dot(factors, vec[:, here], preferred_element_type=F32)
        model = model[:columns] + (model[columns : 2 * columns] + model[2 * columns :])
        applied = levels_at(energies, start, step) * mine[:, here].astype(F32)
        for term in terms:
            applied = applied + term[:, here]
        out[:, here] = applied - model


def last_kernel(first, second, out):
    out[...] = first[...] + second[...]


def call(kernel, name, out_shape, in_specs, out_specs, args, cycles, scratch=(), room=24):
    return pl.pallas_call(
        kernel,
        out_shape=out_shape,
        in_specs=in_specs,
        out_specs=out_specs,
        scratch_shapes=list(scratch),
        compiler_params=pltpu.CompilerParams(vmem_limit_bytes=room * 1024 * 1024),
        cost_estimate=pl.CostEstimate(
            flops=0, bytes_accessed=cycles * 3_000_000, transcendentals=0
        ),
        name=name,
    )(*args)


def on_device(vectors, energies, tile_values, tile_rows, tile_cols, tile_offsets, tile_count):
    columns, rows_dev = vectors.shape
    n_sub = lax.axis_size("sub")
    pair = n_sub == 2
    width = columns * n_sub
    slots, side = tile_values.shape[1:3]
    levels = energies.reshape(rows_dev // side, side)
    narrow = jax.ShapeDtypeStruct((width, rows_dev), BF16)
    block = jax.ShapeDtypeStruct((width, rows_dev), F32)
    half = jax.ShapeDtypeStruct((columns, rows_dev), F32)
    square = jax.ShapeDtypeStruct((2 * width, side), F32)
    parts = [half] * 2 if pair else [block]

    table = jnp.concatenate(
        [tile_rows + LIVE_UNIT * tile_count, tile_cols, tile_offsets], 0
    )
    tiles = call(
        load_kernel,
        "load",
        jax.ShapeDtypeStruct((slots, side, side), BF16),
        [HBM],
        VMEM,
        (tile_values.reshape(slots, side, side),),
        1,
        [pltpu.SemaphoreType.DMA],
        51,
    )
    if pair:
        other = swap_sub(vectors)
        below = shifted(vectors, BW)
        whole = call(join_kernel, "join", narrow, [VMEM] * 3, VMEM, (vectors, other, below), 1)
    else:
        whole = lax.all_gather(vectors, "sub", axis=0, tiled=True)
    m0, m1, m2, before = call(
        mirror_kernel,
        "mirror",
        [block] * 3 + [square],
        [SMEM] + [VMEM] * 3,
        [VMEM] * 4,
        (table, whole, levels, tiles),
        2,
        [pltpu.VMEM((BW + 1, width, rows_dev), F32)],
    )
    if pair:
        whole2, across, m1 = call(
            join_below_kernel,
            "join_below",
            [narrow] * 2 + [block],
            [VMEM] * 4,
            [VMEM] * 3,
            (below, swap_sub(below), whole, m1),
            1,
        )
    else:
        whole2 = shifted(whole, BW)
        across = jnp.where(lax.rem(lax.axis_index("blk"), 2) == 1, whole2, whole)
    whole1 = swap_core(across)
    crossed = swap_core(m1)
    up = call(
        functools.partial(up_kernel, columns),
        "up",
        parts,
        [VMEM] * 2 + [ANY],
        [VMEM] * len(parts),
        (m2, crossed, m2),
        1,
    )
    *own, small = call(
        functools.partial(direct_kernel, columns),
        "direct",
        parts + [square],
        [SMEM] + [VMEM] * 7,
        [VMEM] * (len(parts) + 1),
        (table, whole, whole1, whole2, tiles, m0, crossed, before),
        3,
        [pltpu.VMEM((BW + 1, width, rows_dev), BF16), pltpu.VMEM((width, rows_dev), F32)],
    )
    first, *others = rounds_over("blk")
    rounds = others + [first] + rounds_over("sub")
    stages = [small]
    for one in rounds:
        stages.append(run_rounds(stages[-1], [one]))
    small = stages[-1]
    if pair:
        up = call(
            sum_kernel,
            "sum",
            half,
            [VMEM] * 2 + [ANY],
            VMEM,
            (up[0], swap_sub(up[1]), stages[len(others)]),
            1,
        )
        terms = [own[0], swap_sub(own[1])]
    else:
        up = lax.psum_scatter(up[0], "sub", scatter_dimension=0, tiled=True)
        terms = [lax.psum_scatter(own[0], "sub", scatter_dimension=0, tiled=True)]
    nearly = call(
        model_kernel,
        "model",
        half,
        [VMEM] * (4 + len(terms)),
        VMEM,
        (small, whole, vectors, levels, *terms),
        2,
        [pltpu.VMEM((width, width), F32)],
    )
    return call(last_kernel, "last", half, [VMEM] * 2, VMEM, (nearly, shifted(up, -BW)), 1)


def solution(mesh):
    in_specs = (
        P("sub", "blk"),
        P("blk"),
        P("blk", "sub", None, None),
        P("blk", "sub"),
        P("blk", "sub"),
        P("blk", "sub"),
        P("blk", "sub"),
    )
    out_specs = P("sub", "blk")
    return jax.shard_map(
        on_device, mesh=mesh, in_specs=in_specs, out_specs=out_specs, check_vma=False
    )
```

```python
import functools

import jax
import jax.numpy as jnp
from jax import lax
from jax.experimental import pallas as pl
from jax.experimental.pallas import tpu as pltpu
from jax.sharding import PartitionSpec as P

BW = 2
GROUP = 64
LIVE_UNIT = 65536
F32 = jnp.float32
BF16 = jnp.bfloat16
I32 = jnp.int32
ANY = pl.BlockSpec(memory_space=pl.ANY)
HBM = pl.BlockSpec(memory_space=pltpu.HBM)
VMEM = pl.BlockSpec(memory_space=pltpu.VMEM)
SMEM = pl.BlockSpec(memory_space=pltpu.SMEM)
NT = (((1,), (1,)), ((), ()))


def shifted(value, steps):
    count = lax.axis_size("blk")
    first, last = (max(0, -steps), min(count, count - steps))
    return lax.ppermute(value, "blk", [(source, source + steps) for source in range(first, last)])


def swap_sub(value):
    return lax.ppermute(value, "sub", [(0, 1), (1, 0)])


def swap_core(value):
    return lax.ppermute(value, "blk", [(i, i ^ 1) for i in range(lax.axis_size("blk"))])


def rounds_over(axis):
    count = lax.axis_size(axis)
    rounds, stride = [], 1
    while stride < count:
        rest = count // stride
        radix = next(p for p in range(2, rest + 1) if rest % p == 0)
        rounds.append((axis, stride, radix))
        stride *= radix
    return rounds


def run_rounds(value, rounds):
    for axis, stride, radix in rounds:
        total = value
        for turn in range(1, radix):
            pairs = []
            for source in range(lax.axis_size(axis)):
                digit = (source // stride) % radix
                pairs.append((source, source + ((digit + turn) % radix - digit) * stride))
            total = total + lax.ppermute(value, axis, pairs)
        value = total
    return value


def tile_at(index, side):
    return pl.ds(pl.multiple_of(index * side, side), side)


def split2(value):
    spread = value * 65537.0
    high = spread - (spread - value)
    return high, value - high


def odd_block():
    return lax.rem(lax.axis_index("blk"), 2) == 1


def in_order(own, other, out):
    rows = own.shape[0]
    first = lax.axis_index("sub") == 0

    @pl.when(first)
    def _():
        out[0:rows, :] = own[...]
        out[rows : 2 * rows, :] = other[...]

    @pl.when(jnp.logical_not(first))
    def _():
        out[0:rows, :] = other[...]
        out[rows : 2 * rows, :] = own[...]


def load_kernel(source, target, sem):
    copy = pltpu.make_async_copy(source, target, sem)
    copy.start()
    copy.wait()


def add_terms(table, slots, term_of, total, place, unrolled=False):
    count = table[0, 0] // LIVE_UNIT
    group_size = min(GROUP, slots)

    def add_group(group):
        first = group * group_size
        terms = [term_of(first + lane) for lane in range(group_size)]
        for lane, term in enumerate(terms):
            live = first + lane < count
            total[place(first + lane)] += jnp.where(live, term, 0.0)

    if unrolled and group_size == slots:
        add_group(0)
    else:
        pl.loop(0, pl.cdiv(count, group_size))(add_group)


def join_kernel(own, other, out):
    in_order(own, other, out)


def join_below_kernel(own, other, whole, out, across):
    in_order(own, other, out)
    odd = odd_block()

    @pl.when(odd)
    def _():
        across[...] = out[...]

    @pl.when(jnp.logical_not(odd))
    def _():
        across[...] = whole[...]


def levels_at(energies, start, step):
    side = energies.shape[1]
    rows = [energies[pl.ds((start + i) // side, 1), :] for i in range(0, step, side)]
    return jnp.concatenate(rows, 1)


def mirror_kernel(table, vec, energies, tiles, m0, m1, m2, small, acc):
    side = tiles.shape[-1]
    width, rows_dev = vec.shape
    acc[...] = jnp.zeros_like(acc)

    add_terms(
        table,
        tiles.shape[0],
        lambda slot: jnp.dot(
            vec[:, tile_at(table[0, slot] % LIVE_UNIT, side)], tiles[slot], preferred_element_type=F32
        ),
        acc,
        lambda slot: (table[2, slot], slice(None), tile_at(table[1, slot], side)),
        unrolled=True,
    )
    m0[...] = acc[0]
    m1[...] = acc[1]
    m2[...] = acc[2]
    total = jnp.zeros((width, 3 * width), F32)
    step = 2 * side
    for start in range(0, rows_dev, step):
        v = vec[:, pl.ds(start, step)]
        scaled = split2(levels_at(energies, start, step) * v.astype(F32))
        total += lax.dot_general(
            v,
            jnp.concatenate([v] + [part.astype(BF16) for part in scaled], 0),
            NT,
            preferred_element_type=F32,
        )
    total *= 1.0 / lax.axis_size("sub")
    small[0:width, 0:width] = total[:, :width]
    small[width : 2 * width, 0:width] = total[:, width : 2 * width] + total[:, 2 * width :]


def write_parts(columns, value, targets):
    if len(targets) == 1:
        targets[0][...] = value(slice(None))
        return
    mine = lax.axis_index("sub") * columns
    for start, target in zip((mine, columns - mine), targets):
        target[...] = value(pl.ds(pl.multiple_of(start, columns), columns))


def up_kernel(columns, m2, crossed, ready, *targets):
    odd = odd_block()

    @pl.when(odd)
    def _():
        write_parts(columns, lambda rows: m2[rows, :] + crossed[rows, :], targets)

    @pl.when(jnp.logical_not(odd))
    def _():
        write_parts(columns, lambda rows: m2[rows, :], targets)


def sum_kernel(first, second, ready, out):
    out[...] = first[...] + second[...]


def direct_kernel(
    columns, table, vec, vec1, vec2, tiles, m0, crossed, before, *rest
):
    targets, (small, sources, own) = rest[:-3], rest[-3:]
    side = tiles.shape[-1]
    width, rows_dev = vec.shape
    own[...] = jnp.zeros_like(own)
    sources[0] = vec[...]
    sources[1] = vec1[...]
    sources[2] = vec2[...]

    add_terms(
        table,
        tiles.shape[0],
        lambda slot: lax.dot_general(
            sources[table[2, slot], :, tile_at(table[1, slot], side)],
            tiles[slot],
            NT,
            preferred_element_type=F32,
        ),
        own,
        lambda slot: (slice(None), tile_at(table[0, slot] % LIVE_UNIT, side)),
    )
    left = jnp.zeros((width, 2 * width), F32)
    step = 2 * side
    for start in range(0, rows_dev, step):
        here = pl.ds(start, step)
        v = vec[:, here]
        parts = jnp.concatenate([part.astype(BF16) for part in split2(own[:, here])], 0)
        left += lax.dot_general(v, parts, NT, preferred_element_type=F32)
    cross = left[:, :width] + left[:, width:]
    small[0:width, 0:width] = before[0:width, 0:width]
    small[width : 2 * width, 0:width] = before[width : 2 * width, 0:width] + (
        cross + cross.T
    )
    odd = odd_block()

    @pl.when(odd)
    def _():
        write_parts(columns, lambda part: own[part, :] + m0[part, :], targets)

    @pl.when(jnp.logical_not(odd))
    def _():
        write_parts(
            columns, lambda part: own[part, :] + (m0[part, :] + crossed[part, :]), targets
        )


def eliminate(system):
    width = system.shape[1]
    col_id = lax.broadcasted_iota(I32, system.shape, 1)
    for pivot in range(0, width, 2):
        col0, col1 = [
            jnp.broadcast_to(system[:, i : i + 1], system.shape) for i in (pivot, pivot + 1)
        ]
        row0, row1 = [
            jnp.broadcast_to(system[i : i + 1, :], system.shape) for i in (pivot, pivot + 1)
        ]
        a, c, b, d = [
            jnp.broadcast_to(col[i : i + 1, :], system.shape)
            for col in (col0, col1)
            for i in (pivot, pivot + 1)
        ]
        ratio = b / a
        new1 = (col1 - col0 * ratio) / (d - c * ratio)
        new0 = col0 / a - new1 * (c / a)
        system = system - (new0 * row0 + new1 * row1)
        system = jnp.where(col_id == pivot, new0, jnp.where(col_id == pivot + 1, new1, system))
    return system[width:, :]


def model_kernel(small, vec, mine, energies, *rest):
    terms, (out, coeffs) = rest[:-2], rest[-2:]
    width, rows_dev = vec.shape
    columns = mine.shape[0]
    side = energies.shape[1]
    coeffs[...] = eliminate(small[:, :width])
    wanted = coeffs[pl.ds(lax.axis_index("sub") * columns, columns), :]
    high, rest_of = split2(wanted)
    mid, low = split2(rest_of)
    factors = jnp.concatenate([high, mid, low], 0).astype(BF16)
    step = 8 * side
    for start in range(0, rows_dev, step):
        here = pl.ds(start, step)
        model = jnp.dot(factors, vec[:, here], preferred_element_type=F32)
        model = model[:columns] + (model[columns : 2 * columns] + model[2 * columns :])
        applied = levels_at(energies, start, step) * mine[:, here].astype(F32)
        for term in terms:
            applied = applied + term[:, here]
        out[:, here] = applied - model


def last_kernel(first, second, out):
    out[...] = first[...] + second[...]


def call(kernel, name, out_shape, in_specs, out_specs, args, cycles, scratch=(), room=24, flops=0):
    return pl.pallas_call(
        kernel,
        out_shape=out_shape,
        in_specs=in_specs,
        out_specs=out_specs,
        scratch_shapes=list(scratch),
        compiler_params=pltpu.CompilerParams(vmem_limit_bytes=room * 1024 * 1024),
        cost_estimate=pl.CostEstimate(
            flops=flops, bytes_accessed=cycles * 3_000_000, transcendentals=0
        ),
        name=name,
    )(*args)


def on_device(vectors, energies, tile_values, tile_rows, tile_cols, tile_offsets, tile_count):
    columns, rows_dev = vectors.shape
    n_sub = lax.axis_size("sub")
    pair = n_sub == 2
    width = columns * n_sub
    slots, side = tile_values.shape[1:3]
    levels = energies.reshape(rows_dev // side, side)
    narrow = jax.ShapeDtypeStruct((width, rows_dev), BF16)
    block = jax.ShapeDtypeStruct((width, rows_dev), F32)
    half = jax.ShapeDtypeStruct((columns, rows_dev), F32)
    square = jax.ShapeDtypeStruct((2 * width, side), F32)
    parts = [half] * 2 if pair else [block]

    table = jnp.concatenate(
        [tile_rows + LIVE_UNIT * tile_count, tile_cols, tile_offsets], 0
    )
    tiles = call(
        load_kernel,
        "load",
        jax.ShapeDtypeStruct((slots, side, side), BF16),
        [HBM],
        VMEM,
        (tile_values.reshape(slots, side, side),),
        1,
        [pltpu.SemaphoreType.DMA],
        51,
        20_000_000_000,
    )
    if pair:
        other = swap_sub(vectors)
        below = shifted(vectors, BW)
        whole = call(join_kernel, "join", narrow, [VMEM] * 2, VMEM, (vectors, other), 1)
    else:
        whole = lax.all_gather(vectors, "sub", axis=0, tiled=True)
    m0, m1, m2, before = call(
        mirror_kernel,
        "mirror",
        [block] * 3 + [square],
        [SMEM] + [VMEM] * 3,
        [VMEM] * 4,
        (table, whole, levels, tiles),
        2,
        [pltpu.VMEM((BW + 1, width, rows_dev), F32)],
    )
    if pair:
        whole2, across = call(
            join_below_kernel,
            "join_below",
            [narrow] * 2,
            [VMEM] * 3,
            [VMEM] * 2,
            (below, swap_sub(below), whole),
            1,
            flops=20_000_000_000,
        )
    else:
        whole2 = shifted(whole, BW)
        across = jnp.where(lax.rem(lax.axis_index("blk"), 2) == 1, whole2, whole)
    whole1 = swap_core(across)
    crossed = swap_core(m1)
    up = call(
        functools.partial(up_kernel, columns),
        "up",
        parts,
        [VMEM] * 2 + [ANY],
        [VMEM] * len(parts),
        (m2, crossed, m2),
        1,
    )
    *own, small = call(
        functools.partial(direct_kernel, columns),
        "direct",
        parts + [square],
        [SMEM] + [VMEM] * 7,
        [VMEM] * (len(parts) + 1),
        (table, whole, whole1, whole2, tiles, m0, crossed, before),
        3,
        [pltpu.VMEM((BW + 1, width, rows_dev), BF16), pltpu.VMEM((width, rows_dev), F32)],
    )
    first, *others = rounds_over("blk")
    rounds = others + [first] + rounds_over("sub")
    stages = [small]
    for one in rounds:
        stages.append(run_rounds(stages[-1], [one]))
    small = stages[-1]
    if pair:
        up = call(
            sum_kernel,
            "sum",
            half,
            [VMEM] * 2 + [ANY],
            VMEM,
            (up[0], swap_sub(up[1]), stages[len(others)]),
            1,
        )
        terms = [own[0], swap_sub(own[1])]
    else:
        up = lax.psum_scatter(up[0], "sub", scatter_dimension=0, tiled=True)
        terms = [lax.psum_scatter(own[0], "sub", scatter_dimension=0, tiled=True)]
    nearly = call(
        model_kernel,
        "model",
        half,
        [VMEM] * (4 + len(terms)),
        VMEM,
        (small, whole, vectors, levels, *terms),
        2,
        [pltpu.VMEM((width, width), F32)],
    )
    return call(last_kernel, "last", half, [VMEM] * 2, VMEM, (nearly, shifted(up, -BW)), 1)


def solution(mesh):
    in_specs = (
        P("sub", "blk"),
        P("blk"),
        P("blk", "sub", None, None),
        P("blk", "sub"),
        P("blk", "sub"),
        P("blk", "sub"),
        P("blk", "sub"),
    )
    out_specs = P("sub", "blk")
    return jax.shard_map(
        on_device, mesh=mesh, in_specs=in_specs, out_specs=out_specs, check_vma=False
    )
```

```python
import functools

import jax
import jax.numpy as jnp
from jax import lax
from jax.experimental import pallas as pl
from jax.experimental.pallas import tpu as pltpu
from jax.sharding import PartitionSpec as P

BW = 2
GROUP = 64
LIVE_UNIT = 65536
F32 = jnp.float32
BF16 = jnp.bfloat16
I32 = jnp.int32
ANY = pl.BlockSpec(memory_space=pl.ANY)
HBM = pl.BlockSpec(memory_space=pltpu.HBM)
VMEM = pl.BlockSpec(memory_space=pltpu.VMEM)
SMEM = pl.BlockSpec(memory_space=pltpu.SMEM)
NT = (((1,), (1,)), ((), ()))


def shifted(value, steps):
    count = lax.axis_size("blk")
    first, last = (max(0, -steps), min(count, count - steps))
    return lax.ppermute(value, "blk", [(source, source + steps) for source in range(first, last)])


def swap_sub(value):
    return lax.ppermute(value, "sub", [(0, 1), (1, 0)])


def swap_core(value):
    return lax.ppermute(value, "blk", [(i, i ^ 1) for i in range(lax.axis_size("blk"))])


def rounds_over(axis):
    count = lax.axis_size(axis)
    rounds, stride = [], 1
    while stride < count:
        rest = count // stride
        radix = next(p for p in range(2, rest + 1) if rest % p == 0)
        rounds.append((axis, stride, radix))
        stride *= radix
    return rounds


def run_rounds(value, rounds):
    for axis, stride, radix in rounds:
        total = value
        for turn in range(1, radix):
            pairs = []
            for source in range(lax.axis_size(axis)):
                digit = (source // stride) % radix
                pairs.append((source, source + ((digit + turn) % radix - digit) * stride))
            total = total + lax.ppermute(value, axis, pairs)
        value = total
    return value


def tile_at(index, side):
    return pl.ds(pl.multiple_of(index * side, side), side)


def split2(value):
    spread = value * 65537.0
    high = spread - (spread - value)
    return high, value - high


def odd_block():
    return lax.rem(lax.axis_index("blk"), 2) == 1


def in_order(own, other, out):
    rows = own.shape[0]
    first = lax.axis_index("sub") == 0

    @pl.when(first)
    def _():
        out[0:rows, :] = own[...]
        out[rows : 2 * rows, :] = other[...]

    @pl.when(jnp.logical_not(first))
    def _():
        out[0:rows, :] = other[...]
        out[rows : 2 * rows, :] = own[...]


def load_kernel(source, target, sem):
    copy = pltpu.make_async_copy(source, target, sem)
    copy.start()
    copy.wait()


def add_terms(table, slots, term_of, total, place, unrolled=False):
    count = table[0, 0] // LIVE_UNIT
    group_size = min(GROUP, slots)

    def add_group(group):
        first = group * group_size
        terms = [term_of(first + lane) for lane in range(group_size)]
        for lane, term in enumerate(terms):
            live = first + lane < count
            total[place(first + lane)] += jnp.where(live, term, 0.0)

    if unrolled and group_size == slots:
        add_group(0)
    else:
        pl.loop(0, pl.cdiv(count, group_size))(add_group)


def join_kernel(own, other, out):
    in_order(own, other, out)


def join_below_kernel(own, other, whole, out, across):
    in_order(own, other, out)
    odd = odd_block()

    @pl.when(odd)
    def _():
        across[...] = out[...]

    @pl.when(jnp.logical_not(odd))
    def _():
        across[...] = whole[...]


def levels_at(energies, start, step):
    side = energies.shape[1]
    rows = [energies[pl.ds((start + i) // side, 1), :] for i in range(0, step, side)]
    return jnp.concatenate(rows, 1)


def mirror_kernel(table, vec, energies, tiles, m0, m1, m2, small, acc):
    side = tiles.shape[-1]
    width, rows_dev = vec.shape
    acc[...] = jnp.zeros_like(acc)

    add_terms(
        table,
        tiles.shape[0],
        lambda slot: jnp.dot(
            vec[:, tile_at(table[0, slot] % LIVE_UNIT, side)], tiles[slot], preferred_element_type=F32
        ),
        acc,
        lambda slot: (table[2, slot], slice(None), tile_at(table[1, slot], side)),
        unrolled=True,
    )
    m0[...] = acc[0]
    m1[...] = acc[1]
    m2[...] = acc[2]
    total = jnp.zeros((width, 3 * width), F32)
    step = 2 * side
    for start in range(0, rows_dev, step):
        v = vec[:, pl.ds(start, step)]
        scaled = split2(levels_at(energies, start, step) * v.astype(F32))
        total += lax.dot_general(
            v,
            jnp.concatenate([v] + [part.astype(BF16) for part in scaled], 0),
            NT,
            preferred_element_type=F32,
        )
    total *= 1.0 / lax.axis_size("sub")
    small[0:width, 0:width] = total[:, :width]
    small[width : 2 * width, 0:width] = total[:, width : 2 * width] + total[:, 2 * width :]


def write_parts(columns, value, targets):
    if len(targets) == 1:
        targets[0][...] = value(slice(None))
        return
    mine = lax.axis_index("sub") * columns
    for start, target in zip((mine, columns - mine), targets):
        target[...] = value(pl.ds(pl.multiple_of(start, columns), columns))


def up_kernel(columns, m2, crossed, ready, *targets):
    odd = odd_block()

    @pl.when(odd)
    def _():
        write_parts(columns, lambda rows: m2[rows, :] + crossed[rows, :], targets)

    @pl.when(jnp.logical_not(odd))
    def _():
        write_parts(columns, lambda rows: m2[rows, :], targets)


def sum_kernel(first, second, ready, out):
    out[...] = first[...] + second[...]


def direct_kernel(
    columns, table, vec, vec1, vec2, tiles, m0, crossed, before, *rest
):
    targets, (small, sources, own) = rest[:-3], rest[-3:]
    side = tiles.shape[-1]
    width, rows_dev = vec.shape
    own[...] = jnp.zeros_like(own)
    sources[0] = vec[...]
    sources[1] = vec1[...]
    sources[2] = vec2[...]

    add_terms(
        table,
        tiles.shape[0],
        lambda slot: lax.dot_general(
            sources[table[2, slot], :, tile_at(table[1, slot], side)],
            tiles[slot],
            NT,
            preferred_element_type=F32,
        ),
        own,
        lambda slot: (slice(None), tile_at(table[0, slot] % LIVE_UNIT, side)),
    )
    left = jnp.zeros((width, 2 * width), F32)
    step = 2 * side
    for start in range(0, rows_dev, step):
        here = pl.ds(start, step)
        v = vec[:, here]
        parts = jnp.concatenate([part.astype(BF16) for part in split2(own[:, here])], 0)
        left += lax.dot_general(v, parts, NT, preferred_element_type=F32)
    cross = left[:, :width] + left[:, width:]
    small[0:width, 0:width] = before[0:width, 0:width]
    small[width : 2 * width, 0:width] = before[width : 2 * width, 0:width] + (
        cross + cross.T
    )
    odd = odd_block()

    @pl.when(odd)
    def _():
        write_parts(columns, lambda part: own[part, :] + m0[part, :], targets)

    @pl.when(jnp.logical_not(odd))
    def _():
        write_parts(
            columns, lambda part: own[part, :] + (m0[part, :] + crossed[part, :]), targets
        )


def eliminate(system):
    width = system.shape[1]
    col_id = lax.broadcasted_iota(I32, system.shape, 1)
    for pivot in range(0, width, 2):
        col0, col1 = [
            jnp.broadcast_to(system[:, i : i + 1], system.shape) for i in (pivot, pivot + 1)
        ]
        row0, row1 = [
            jnp.broadcast_to(system[i : i + 1, :], system.shape) for i in (pivot, pivot + 1)
        ]
        a, c, b, d = [
            jnp.broadcast_to(col[i : i + 1, :], system.shape)
            for col in (col0, col1)
            for i in (pivot, pivot + 1)
        ]
        ratio = b / a
        new1 = (col1 - col0 * ratio) / (d - c * ratio)
        new0 = col0 / a - new1 * (c / a)
        system = system - (new0 * row0 + new1 * row1)
        system = jnp.where(col_id == pivot, new0, jnp.where(col_id == pivot + 1, new1, system))
    return system[width:, :]


def model_kernel(small, vec, mine, energies, *rest):
    terms, out = rest[:-1], rest[-1]
    width, rows_dev = vec.shape
    columns = mine.shape[0]
    side = energies.shape[1]
    own = pl.ds(width + lax.axis_index("sub") * columns, columns)
    wanted = eliminate(jnp.concatenate([small[0:width, :], small[own, :]], 0)[:, :width])
    high, rest_of = split2(wanted)
    mid, low = split2(rest_of)
    factors = jnp.concatenate([high, mid, low], 0).astype(BF16)
    step = 8 * side
    for start in range(0, rows_dev, step):
        here = pl.ds(start, step)
        model = jnp.dot(factors, vec[:, here], preferred_element_type=F32)
        model = model[:columns] + (model[columns : 2 * columns] + model[2 * columns :])
        applied = levels_at(energies, start, step) * mine[:, here].astype(F32)
        for term in terms:
            applied = applied + term[:, here]
        out[:, here] = applied - model


def call(kernel, name, out_shape, in_specs, out_specs, args, cycles, scratch=(), room=24, flops=0):
    return pl.pallas_call(
        kernel,
        out_shape=out_shape,
        in_specs=in_specs,
        out_specs=out_specs,
        scratch_shapes=list(scratch),
        compiler_params=pltpu.CompilerParams(vmem_limit_bytes=room * 1024 * 1024),
        cost_estimate=pl.CostEstimate(
            flops=flops, bytes_accessed=cycles * 3_000_000, transcendentals=0
        ),
        name=name,
    )(*args)


def on_device(vectors, energies, tile_values, tile_rows, tile_cols, tile_offsets, tile_count):
    columns, rows_dev = vectors.shape
    n_sub = lax.axis_size("sub")
    pair = n_sub == 2
    width = columns * n_sub
    slots, side = tile_values.shape[1:3]
    levels = energies.reshape(rows_dev // side, side)
    narrow = jax.ShapeDtypeStruct((width, rows_dev), BF16)
    block = jax.ShapeDtypeStruct((width, rows_dev), F32)
    half = jax.ShapeDtypeStruct((columns, rows_dev), F32)
    square = jax.ShapeDtypeStruct((2 * width, side), F32)
    parts = [half] * 2 if pair else [block]

    table = jnp.concatenate(
        [tile_rows + LIVE_UNIT * tile_count, tile_cols, tile_offsets], 0
    )
    tiles = call(
        load_kernel,
        "load",
        jax.ShapeDtypeStruct((slots, side, side), BF16),
        [HBM],
        VMEM,
        (tile_values.reshape(slots, side, side),),
        1,
        [pltpu.SemaphoreType.DMA],
        51,
        20_000_000_000,
    )
    if pair:
        other = swap_sub(vectors)
        below = shifted(vectors, BW)
        whole = call(join_kernel, "join", narrow, [VMEM] * 2, VMEM, (vectors, other), 1)
    else:
        whole = lax.all_gather(vectors, "sub", axis=0, tiled=True)
    m0, m1, m2, before = call(
        mirror_kernel,
        "mirror",
        [block] * 3 + [square],
        [SMEM] + [VMEM] * 3,
        [VMEM] * 4,
        (table, whole, levels, tiles),
        2,
        [pltpu.VMEM((BW + 1, width, rows_dev), F32)],
    )
    if pair:
        whole2, across = call(
            join_below_kernel,
            "join_below",
            [narrow] * 2,
            [VMEM] * 3,
            [VMEM] * 2,
            (below, swap_sub(below), whole),
            1,
            flops=20_000_000_000,
        )
    else:
        whole2 = shifted(whole, BW)
        across = jnp.where(lax.rem(lax.axis_index("blk"), 2) == 1, whole2, whole)
    whole1 = swap_core(across)
    crossed = swap_core(m1)
    up = call(
        functools.partial(up_kernel, columns),
        "up",
        parts,
        [VMEM] * 2 + [ANY],
        [VMEM] * len(parts),
        (m2, crossed, m2),
        1,
    )
    *own, small = call(
        functools.partial(direct_kernel, columns),
        "direct",
        parts + [square],
        [SMEM] + [VMEM] * 7,
        [VMEM] * (len(parts) + 1),
        (table, whole, whole1, whole2, tiles, m0, crossed, before),
        3,
        [pltpu.VMEM((BW + 1, width, rows_dev), BF16), pltpu.VMEM((width, rows_dev), F32)],
    )
    first, *others = rounds_over("blk")
    rounds = others + [first] + rounds_over("sub")
    stages = [small]
    for one in rounds:
        stages.append(run_rounds(stages[-1], [one]))
    small = stages[-1]
    if pair:
        up = call(
            sum_kernel,
            "sum",
            half,
            [VMEM] * 2 + [ANY],
            VMEM,
            (up[0], swap_sub(up[1]), stages[len(others)]),
            1,
        )
        terms = [own[0], swap_sub(own[1])]
    else:
        up = lax.psum_scatter(up[0], "sub", scatter_dimension=0, tiled=True)
        terms = [lax.psum_scatter(own[0], "sub", scatter_dimension=0, tiled=True)]
    nearly = call(
        model_kernel,
        "model",
        half,
        [VMEM] * (4 + len(terms)),
        VMEM,
        (small, whole, vectors, levels, *terms),
        2,
    )
    return nearly + shifted(up, -BW)


def solution(mesh):
    in_specs = (
        P("sub", "blk"),
        P("blk"),
        P("blk", "sub", None, None),
        P("blk", "sub"),
        P("blk", "sub"),
        P("blk", "sub"),
        P("blk", "sub"),
    )
    out_specs = P("sub", "blk")
    return jax.shard_map(
        on_device, mesh=mesh, in_specs=in_specs, out_specs=out_specs, check_vma=False
    )
```

```python
import functools

import jax
import jax.numpy as jnp
from jax import lax
from jax.experimental import pallas as pl
from jax.experimental.pallas import tpu as pltpu
from jax.sharding import PartitionSpec as P

BW = 2
GROUP = 64
LIVE_UNIT = 65536
F32 = jnp.float32
BF16 = jnp.bfloat16
I32 = jnp.int32
ANY = pl.BlockSpec(memory_space=pl.ANY)
HBM = pl.BlockSpec(memory_space=pltpu.HBM)
VMEM = pl.BlockSpec(memory_space=pltpu.VMEM)
SMEM = pl.BlockSpec(memory_space=pltpu.SMEM)
NT = (((1,), (1,)), ((), ()))


def shifted(value, steps):
    count = lax.axis_size("blk")
    first, last = (max(0, -steps), min(count, count - steps))
    return lax.ppermute(value, "blk", [(source, source + steps) for source in range(first, last)])


def swap_sub(value):
    return lax.ppermute(value, "sub", [(0, 1), (1, 0)])


def swap_core(value):
    return lax.ppermute(value, "blk", [(i, i ^ 1) for i in range(lax.axis_size("blk"))])


def rounds_over(axis):
    count = lax.axis_size(axis)
    rounds, stride = [], 1
    while stride < count:
        rest = count // stride
        radix = next(p for p in range(2, rest + 1) if rest % p == 0)
        rounds.append((axis, stride, radix))
        stride *= radix
    return rounds


def run_rounds(value, rounds):
    for axis, stride, radix in rounds:
        total = value
        for turn in range(1, radix):
            pairs = []
            for source in range(lax.axis_size(axis)):
                digit = (source // stride) % radix
                pairs.append((source, source + ((digit + turn) % radix - digit) * stride))
            total = total + lax.ppermute(value, axis, pairs)
        value = total
    return value


def tile_at(index, side):
    return pl.ds(pl.multiple_of(index * side, side), side)


def split2(value):
    spread = value * 65537.0
    high = spread - (spread - value)
    return high, value - high


def odd_block():
    return lax.rem(lax.axis_index("blk"), 2) == 1


def in_order(own, other, out):
    rows = own.shape[0]
    first = lax.axis_index("sub") == 0

    @pl.when(first)
    def _():
        out[0:rows, :] = own[...]
        out[rows : 2 * rows, :] = other[...]

    @pl.when(jnp.logical_not(first))
    def _():
        out[0:rows, :] = other[...]
        out[rows : 2 * rows, :] = own[...]


def load_kernel(source, target, sem):
    copy = pltpu.make_async_copy(source, target, sem)
    copy.start()
    copy.wait()


def add_terms(table, slots, term_of, total, place, unrolled=False):
    count = table[0, 0] // LIVE_UNIT
    group_size = min(GROUP, slots)

    def add_group(group):
        first = group * group_size
        terms = [term_of(first + lane) for lane in range(group_size)]
        for lane, term in enumerate(terms):
            live = first + lane < count
            total[place(first + lane)] += jnp.where(live, term, 0.0)

    if unrolled and group_size == slots:
        add_group(0)
    else:
        pl.loop(0, pl.cdiv(count, group_size))(add_group)


def join_kernel(own, other, out):
    in_order(own, other, out)


def join_below_kernel(own, other, whole, out, across):
    in_order(own, other, out)
    odd = odd_block()

    @pl.when(odd)
    def _():
        across[...] = out[...]

    @pl.when(jnp.logical_not(odd))
    def _():
        across[...] = whole[...]


def levels_at(energies, start, step):
    side = energies.shape[1]
    rows = [energies[pl.ds((start + i) // side, 1), :] for i in range(0, step, side)]
    return jnp.concatenate(rows, 1)


def mirror_kernel(table, vec, energies, tiles, m0, m1, m2, small, acc):
    side = tiles.shape[-1]
    width, rows_dev = vec.shape
    acc[...] = jnp.zeros_like(acc)

    add_terms(
        table,
        tiles.shape[0],
        lambda slot: jnp.dot(
            vec[:, tile_at(table[0, slot] % LIVE_UNIT, side)], tiles[slot], preferred_element_type=F32
        ),
        acc,
        lambda slot: (table[2, slot], slice(None), tile_at(table[1, slot], side)),
        unrolled=True,
    )
    m0[...] = acc[0]
    m1[...] = acc[1]
    m2[...] = acc[2]
    total = jnp.zeros((width, 3 * width), F32)
    step = 2 * side
    for start in range(0, rows_dev, step):
        v = vec[:, pl.ds(start, step)]
        scaled = split2(levels_at(energies, start, step) * v.astype(F32))
        total += lax.dot_general(
            v,
            jnp.concatenate([v] + [part.astype(BF16) for part in scaled], 0),
            NT,
            preferred_element_type=F32,
        )
    total *= 1.0 / lax.axis_size("sub")
    small[0:width, 0:width] = total[:, :width]
    small[width : 2 * width, 0:width] = total[:, width : 2 * width] + total[:, 2 * width :]


def write_parts(columns, value, targets):
    if len(targets) == 1:
        targets[0][...] = value(slice(None))
        return
    mine = lax.axis_index("sub") * columns
    for start, target in zip((mine, columns - mine), targets):
        target[...] = value(pl.ds(pl.multiple_of(start, columns), columns))


def up_kernel(columns, m2, crossed, ready, *targets):
    odd = odd_block()

    @pl.when(odd)
    def _():
        write_parts(columns, lambda rows: m2[rows, :] + crossed[rows, :], targets)

    @pl.when(jnp.logical_not(odd))
    def _():
        write_parts(columns, lambda rows: m2[rows, :], targets)


def sum_kernel(first, second, ready, out):
    out[...] = first[...] + second[...]


def direct_kernel(
    columns, table, vec, vec1, vec2, tiles, m0, crossed, before, *rest
):
    targets, (small, sources, own) = rest[:-3], rest[-3:]
    side = tiles.shape[-1]
    width, rows_dev = vec.shape
    own[...] = jnp.zeros_like(own)
    sources[0] = vec[...]
    sources[1] = vec1[...]
    sources[2] = vec2[...]

    add_terms(
        table,
        tiles.shape[0],
        lambda slot: lax.dot_general(
            sources[table[2, slot], :, tile_at(table[1, slot], side)],
            tiles[slot],
            NT,
            preferred_element_type=F32,
        ),
        own,
        lambda slot: (slice(None), tile_at(table[0, slot] % LIVE_UNIT, side)),
    )
    left = jnp.zeros((width, 2 * width), F32)
    step = 2 * side
    for start in range(0, rows_dev, step):
        here = pl.ds(start, step)
        v = vec[:, here]
        parts = jnp.concatenate([part.astype(BF16) for part in split2(own[:, here])], 0)
        left += lax.dot_general(v, parts, NT, preferred_element_type=F32)
    cross = left[:, :width] + left[:, width:]
    small[0:width, 0:width] = before[0:width, 0:width]
    small[width : 2 * width, 0:width] = before[width : 2 * width, 0:width] + (
        cross + cross.T
    )
    odd = odd_block()

    @pl.when(odd)
    def _():
        write_parts(columns, lambda part: own[part, :] + m0[part, :], targets)

    @pl.when(jnp.logical_not(odd))
    def _():
        write_parts(
            columns, lambda part: own[part, :] + (m0[part, :] + crossed[part, :]), targets
        )


def eliminate(system):
    width = system.shape[1]
    col_id = lax.broadcasted_iota(I32, system.shape, 1)
    for pivot in range(0, width, 2):
        col0, col1 = [
            jnp.broadcast_to(system[:, i : i + 1], system.shape) for i in (pivot, pivot + 1)
        ]
        row0, row1 = [
            jnp.broadcast_to(system[i : i + 1, :], system.shape) for i in (pivot, pivot + 1)
        ]
        a, c, b, d = [
            jnp.broadcast_to(col[i : i + 1, :], system.shape)
            for col in (col0, col1)
            for i in (pivot, pivot + 1)
        ]
        ratio = b / a
        new1 = (col1 - col0 * ratio) / (d - c * ratio)
        new0 = col0 / a - new1 * (c / a)
        system = system - (new0 * row0 + new1 * row1)
        system = jnp.where(col_id == pivot, new0, jnp.where(col_id == pivot + 1, new1, system))
    return system[width:, :]


def model_kernel(small, vec, mine, energies, *rest):
    terms, (out, coeffs) = rest[:-2], rest[-2:]
    width, rows_dev = vec.shape
    columns = mine.shape[0]
    side = energies.shape[1]
    coeffs[...] = eliminate(small[:, :width])
    wanted = coeffs[pl.ds(lax.axis_index("sub") * columns, columns), :]
    high, rest_of = split2(wanted)
    mid, low = split2(rest_of)
    factors = jnp.concatenate([high, mid, low], 0).astype(BF16)
    step = 8 * side
    for start in range(0, rows_dev, step):
        here = pl.ds(start, step)
        model = jnp.dot(factors, vec[:, here], preferred_element_type=F32)
        model = model[:columns] + (model[columns : 2 * columns] + model[2 * columns :])
        applied = levels_at(energies, start, step) * mine[:, here].astype(F32)
        for term in terms:
            applied = applied + term[:, here]
        out[:, here] = applied - model


def last_kernel(first, second, out):
    out[...] = first[...] + second[...]


def call(kernel, name, out_shape, in_specs, out_specs, args, cycles, scratch=(), room=24, flops=0):
    return pl.pallas_call(
        kernel,
        out_shape=out_shape,
        in_specs=in_specs,
        out_specs=out_specs,
        scratch_shapes=list(scratch),
        compiler_params=pltpu.CompilerParams(vmem_limit_bytes=room * 1024 * 1024),
        cost_estimate=pl.CostEstimate(
            flops=flops, bytes_accessed=cycles * 3_000_000, transcendentals=0
        ),
        name=name,
    )(*args)


def on_device(vectors, energies, tile_values, tile_rows, tile_cols, tile_offsets, tile_count):
    columns, rows_dev = vectors.shape
    n_sub = lax.axis_size("sub")
    pair = n_sub == 2
    width = columns * n_sub
    slots, side = tile_values.shape[1:3]
    levels = energies.reshape(rows_dev // side, side)
    narrow = jax.ShapeDtypeStruct((width, rows_dev), BF16)
    block = jax.ShapeDtypeStruct((width, rows_dev), F32)
    half = jax.ShapeDtypeStruct((columns, rows_dev), F32)
    square = jax.ShapeDtypeStruct((2 * width, side), F32)
    parts = [half] * 2 if pair else [block]

    table = jnp.concatenate(
        [tile_rows + LIVE_UNIT * tile_count, tile_cols, tile_offsets], 0
    )
    tiles = call(
        load_kernel,
        "load",
        jax.ShapeDtypeStruct((slots, side, side), BF16),
        [HBM],
        VMEM,
        (tile_values.reshape(slots, side, side),),
        1,
        [pltpu.SemaphoreType.DMA],
        51,
        2000000000,
    )
    if pair:
        other = swap_sub(vectors)
        below = shifted(vectors, BW)
        whole = call(join_kernel, "join", narrow, [VMEM] * 2, VMEM, (vectors, other), 1)
    else:
        whole = lax.all_gather(vectors, "sub", axis=0, tiled=True)
    m0, m1, m2, before = call(
        mirror_kernel,
        "mirror",
        [block] * 3 + [square],
        [SMEM] + [VMEM] * 3,
        [VMEM] * 4,
        (table, whole, levels, tiles),
        2,
        [pltpu.VMEM((BW + 1, width, rows_dev), F32)],
        flops=20000000000,
    )
    if pair:
        whole2, across = call(
            join_below_kernel,
            "join_below",
            [narrow] * 2,
            [VMEM] * 3,
            [VMEM] * 2,
            (below, swap_sub(below), whole),
            1,
            flops=20000000000,
        )
    else:
        whole2 = shifted(whole, BW)
        across = jnp.where(lax.rem(lax.axis_index("blk"), 2) == 1, whole2, whole)
    whole1 = swap_core(across)
    crossed = swap_core(m1)
    up = call(
        functools.partial(up_kernel, columns),
        "up",
        parts,
        [VMEM] * 2 + [ANY],
        [VMEM] * len(parts),
        (m2, crossed, m2),
        1,
    )
    *own, small = call(
        functools.partial(direct_kernel, columns),
        "direct",
        parts + [square],
        [SMEM] + [VMEM] * 7,
        [VMEM] * (len(parts) + 1),
        (table, whole, whole1, whole2, tiles, m0, crossed, before),
        3,
        [pltpu.VMEM((BW + 1, width, rows_dev), BF16), pltpu.VMEM((width, rows_dev), F32)],
    )
    first, *others = rounds_over("blk")
    rounds = others + [first] + rounds_over("sub")
    stages = [small]
    for one in rounds:
        stages.append(run_rounds(stages[-1], [one]))
    small = stages[-1]
    if pair:
        up = call(
            sum_kernel,
            "sum",
            half,
            [VMEM] * 2 + [ANY],
            VMEM,
            (up[0], swap_sub(up[1]), stages[len(others)]),
            1,
        )
        terms = [own[0], swap_sub(own[1])]
    else:
        up = lax.psum_scatter(up[0], "sub", scatter_dimension=0, tiled=True)
        terms = [lax.psum_scatter(own[0], "sub", scatter_dimension=0, tiled=True)]
    nearly = call(
        model_kernel,
        "model",
        half,
        [VMEM] * (4 + len(terms)),
        VMEM,
        (small, whole, vectors, levels, *terms),
        2,
        [pltpu.VMEM((width, width), F32)],
    )
    return call(last_kernel, "last", half, [VMEM] * 2, VMEM, (nearly, shifted(up, -BW)), 1)


def solution(mesh):
    in_specs = (
        P("sub", "blk"),
        P("blk"),
        P("blk", "sub", None, None),
        P("blk", "sub"),
        P("blk", "sub"),
        P("blk", "sub"),
        P("blk", "sub"),
    )
    out_specs = P("sub", "blk")
    return jax.shard_map(
        on_device, mesh=mesh, in_specs=in_specs, out_specs=out_specs, check_vma=False
    )
```
